512 devices in a mesh: dp: 32 (over x, y), expert: 2 (over core), ffn: 8 (over z).
Axes of the slice: x: 4, y: 8, z: 8, core: 2. Of those that a mesh axis runs over, the one named last changes fastest.
Arguments:
- grad_rows: bfloat16 [4096, 6144], P('dp', 'ffn'), may hold values from -80 to 80
- gate_probs: float32 [4096, 2], P('dp'), may hold values from 0.1 to 1
- expert_ids: int32 [4096, 2], P('dp'), may hold values from 0 to 3, all different within a row; in each aligned block of 128 rows (0 to 127, 128 to 255, ...) at most 72 rows name the same one
- gate_pre: bfloat16 [4, 2304, 8192], P('expert', 'ffn', 'dp'), may hold values from -6 to 6
- up_pre: bfloat16 [4, 2304, 8192], P('expert', 'ffn', 'dp'), may hold values from -40 to 40
- down_weight: bfloat16 [4, 8192, 6144], P('expert', 'dp', 'ffn'), may hold values from -0.0625 to 0.0625
Outputs:
- down_grad: bfloat16 [4, 8192, 6144], P('expert', 'dp', 'ffn')
- gate_grad: bfloat16 [4, 2304, 8192], P('expert', 'ffn', 'dp')
- up_grad: bfloat16 [4, 2304, 8192], P('expert', 'ffn', 'dp')
The draws below stay inside these ranges and needn't reach their ends.
Inputs may be any that keep to these rules, and one draw needn't show every extreme that they name: `expert_ids`: in the 128 tokens of one index of dp no expert is named by more than 72 routes, a bound that some block reaches; a token's two routes name different experts.
All inputs are finite; a program needn't handle non-finite values.
Results may differ from the reference program's by a relative error of at most 0.019.
Values may be sent and summed in bfloat16 or wider, within the bound.
No kernel may reach another device: no remote copies, remote signals or barrier semaphores. Data moves between devices by JAX's collectives and lax.ppermute only.
A program may use at most 64 MiB of HBM per device.

```python
import math
import jax
import jax.numpy as jnp
import numpy as np
from jax import lax

D = 6144
FF = 8192
TOP = 2
TOK_DEV = 128
EXPERTS = 4
CAP = 72
ROWS = 2304
TOKENS = 4096
N_DP = 32
N_FFN = 8


def draw_grad_rows(key, part):
    key_values, key_scale = jax.random.split(key, 2)
    position = jnp.arange(TOKENS, dtype=jnp.float32) / TOKENS
    row_scale = 0.4 * jnp.power(3.0, position) * jnp.power(10.0, jax.random.uniform(key_scale, (TOKENS,), jnp.float32))
    values_drawn = jax.random.normal(key_values, (TOKENS, D), jnp.float32)
    values_drawn = jnp.clip(values_drawn, -6.0, 6.0)
    return (row_scale[:, None] * values_drawn).astype(jnp.bfloat16)


def draw_up_pre(key, part):
    key_values = jax.random.fold_in(jax.random.fold_in(key, 17), 0)
    position = jnp.arange(FF, dtype=jnp.float32) / FF
    column_scale = 0.3 * jnp.power(10.0, position)
    values_drawn = jnp.clip(jax.random.normal(key_values, (EXPERTS, ROWS, FF), jnp.float32), -6.0, 6.0)
    return (column_scale[None, None, :] * values_drawn).astype(jnp.bfloat16)


def block_levels(stream_key, dims, cuts, low, largest):
    gain = 1.0
    for dim, shards_of in cuts:
        steps = jax.random.uniform(jax.random.fold_in(jax.random.fold_in(stream_key, 6), dim), (shards_of,), jnp.float32, low / len(cuts), largest / len(cuts))
        gain = gain * jnp.repeat(jnp.exp(steps), dims[dim] // shards_of).reshape((-1,) + (1,) * (len(dims) - 1 - dim))
    return gain


def routed_block(own_key, own, number, rows, count, top, most, slope):
    sequence = jax.random.permutation(own_key, count)
    crowded, ordinary = portions_of(count, rows * top, most, slope, True), portions_of(count, rows * top, most, slope, False)
    places = jnp.arange(count)

    def named(sizes, rotation):
        used = int((sizes > 0).sum())
        fixed = max(1, used // 4)
        shifted = fixed + (places - fixed + rotation * (used - fixed)) % max(1, count - fixed)
        return jnp.zeros((count,), jnp.int32).at[sequence[jnp.where(places < fixed, places, shifted)]].set(jnp.asarray(sizes, jnp.int32))

    sizes = jnp.where(number % 4 == 0, named(crowded, number // 4), named(ordinary, number - number // 4 - 1))
    mixed = jax.random.permutation(jax.random.fold_in(own, 3), count)
    giver, taker = mixed[0:count // 2 * 2:2], mixed[1:count // 2 * 2:2]
    room = jnp.minimum(sizes[giver] - 1, most - sizes[taker]) // 2
    room = jnp.where((giver == sequence[0]) | (taker == sequence[0]) | (sizes[taker] == 0), 0, jnp.maximum(room, 0))
    shifted = jax.random.randint(jax.random.fold_in(own, 4), (count // 2,), 0, 1 << 20) % (room + 1)
    sizes = sizes.at[giver].add(-shifted).at[taker].add(shifted)
    members = jnp.searchsorted(jnp.cumsum(sizes), jnp.arange(rows * top), side="right").astype(jnp.int32)
    listing = members.reshape(top, rows).T
    listing = listing[jax.random.permutation(jax.random.fold_in(own, 1), rows)]
    rotation = jax.random.randint(jax.random.fold_in(own, 2), (rows, 1), 0, top)
    return jnp.take_along_axis(listing, (jnp.arange(top)[None, :] + rotation) % top, axis=1)


def portions_of(count, total, most, slope, full):
    weights = [(1 << 20) // math.isqrt(grade ** slope) + 1 for grade in range(1, count + 1)]
    largest = most if full else min(most, max(-(-total // count), total * weights[0] // sum(weights)))
    least = 1 if total - largest >= count - 1 else 0
    counts, rest = [largest] + [least] * (count - 1), total - largest - least * (count - 1)
    while rest > 0:
        movable = [i for i in range(1, count) if counts[i] < largest] or [i for i in range(1, count) if counts[i] < most]
        pool, budget = sum([weights[i] for i in movable]), rest
        for i in movable:
            addition = min(most - counts[i], max(1, budget * weights[i] // pool), rest)
            counts[i] = counts[i] + addition
            rest = rest - addition
    return np.array(counts)


def noise(stream_key, dims, deviation, limit, cuts=(), held_as=jnp.bfloat16):
    drawn = jax.random.normal(stream_key, dims, jnp.float32) * deviation
    if len(cuts) > 0:
        drawn = block_levels(stream_key, dims, cuts, -0.22, 0.18) * drawn
    return jnp.clip(drawn, min=-limit, max=limit).astype(held_as)


def setup_inputs(seed: int = 0) -> dict:
    key_of = jax.random.split(jax.random.key(seed), 7)
    grad_rows = draw_grad_rows(jax.random.fold_in(key_of[6], 71), 0)
    gate_probs = jnp.clip(0.1 + 0.9 * jax.random.uniform(key_of[1], (TOKENS, TOP), jnp.float32) ** block_levels(key_of[1], (TOKENS, TOP), ((0, 32),), -0.2, 0.2), 0.1, 1.0)
    expert_ids_keys = jax.random.split(jax.random.fold_in(key_of[2], 1), TOKENS // TOK_DEV)
    expert_ids_turns = jax.random.permutation(jax.random.fold_in(key_of[2], 3), TOKENS // TOK_DEV)
    expert_ids = jax.vmap(lambda own, number: routed_block(jax.random.fold_in(key_of[2], 2), own, number, TOK_DEV, EXPERTS, TOP, CAP, 2))(expert_ids_keys, expert_ids_turns).reshape((TOKENS, TOP))
    gate_pre = noise(key_of[3], (EXPERTS, ROWS, FF), 1.0, 6.0, ((0, 2), (1, 8), (2, 32)))
    up_pre = draw_up_pre(jax.random.fold_in(key_of[6], 71), 0)
    down_weight = noise(key_of[5], (EXPERTS, FF, D), FF ** -0.5, 0.0625, ((0, 2), (1, 32), (2, 8)))
    return {"grad_rows": grad_rows, "gate_probs": gate_probs, "expert_ids": expert_ids, "gate_pre": gate_pre, "up_pre": up_pre, "down_weight": down_weight}


def slot_table(expert_ids):
    route_ids = expert_ids.reshape(N_DP, TOK_DEV * TOP)
    one_hot = (route_ids[:, :, None] == jnp.arange(EXPERTS, dtype=jnp.int32)[None, None, :]).astype(jnp.int32)
    earlier = jnp.cumsum(one_hot, axis=1) - one_hot
    return lax.optimization_barrier(jnp.sum(earlier * one_hot, axis=2)).reshape(TOKENS, TOP).astype(jnp.int32)

def reference(grad_rows, gate_probs, expert_ids, gate_pre, up_pre, down_weight):
    slot_index = slot_table(expert_ids)
    source = (jnp.arange(TOKENS, dtype=jnp.int32) // TOK_DEV).astype(jnp.int32)
    row_index = (source[:, None] * CAP + slot_index).astype(jnp.int32)
    scaled = gate_probs[:, :, None] * grad_rows.astype(jnp.float32)[:, None, :]
    dispatched = jnp.zeros((EXPERTS, ROWS, D), jnp.float32).at[expert_ids, row_index].add(scaled)
    dispatched = dispatched.astype(jnp.bfloat16)
    gate_value = gate_pre.astype(jnp.float32)
    up_value = up_pre.astype(jnp.float32)
    sigmoid_gate = jax.nn.sigmoid(gate_value)
    silu_gate = gate_value * sigmoid_gate
    hidden = (silu_gate * up_value).astype(jnp.bfloat16)
    block_width = D // N_FFN
    hidden_grad = jnp.zeros((EXPERTS, ROWS, FF), jnp.float32)
    for block in range(N_FFN):
        lower = block * block_width
        term = jnp.einsum('erd,efd->erf', dispatched[:, :, lower:lower + block_width].astype(jnp.float32), down_weight[:, :, lower:lower + block_width].astype(jnp.float32))
        rounded = lax.optimization_barrier(term.astype(jnp.bfloat16))
        hidden_grad = hidden_grad + rounded.astype(jnp.float32)
    gate_grad = (hidden_grad * up_value * sigmoid_gate * (1.0 + gate_value * (1.0 - sigmoid_gate))).astype(jnp.bfloat16)
    up_grad = (hidden_grad * silu_gate).astype(jnp.bfloat16)
    weight_grad = jnp.einsum('erf,erd->efd', hidden.astype(jnp.float32), dispatched.astype(jnp.float32))
    squares = jnp.sum(jnp.square(weight_grad))
    clip_limit = jnp.float32(0.5 * (float(EXPERTS) * float(FF) * float(D)) ** 0.5)
    factor = clip_limit / jnp.maximum(jnp.sqrt(squares), clip_limit)
    down_grad = (weight_grad * factor).astype(jnp.bfloat16)
    return (down_grad, gate_grad, up_grad)
```

```python
import math

import jax
import jax.numpy as jnp
from jax import lax
from jax.experimental import pallas as pl
from jax.experimental.pallas import tpu as pltpu
from jax.sharding import PartitionSpec as P

CAP = 72
META = 8


def hidden_kernel(gate_ref, up_ref, hidden_ref):
    gate = gate_ref[...].astype(jnp.float32)
    up = up_ref[...].astype(jnp.float32)
    hidden_ref[0] = (gate * jax.nn.sigmoid(gate) * up).astype(jnp.bfloat16)


def hidden_copies(gate_pre, up_pre, copies):
    return pl.pallas_call(
        hidden_kernel,
        grid=(copies,),
        in_specs=[pl.BlockSpec(gate_pre.shape, lambda i: (0, 0, 0))] * 2,
        out_specs=pl.BlockSpec((1,) + gate_pre.shape, lambda i: (i, 0, 0, 0)),
        out_shape=jax.ShapeDtypeStruct((copies,) + gate_pre.shape, jnp.bfloat16),
        name="hidden_copies",
    )(gate_pre, up_pre)


def gate_up_kernel(grad_ref, gate_ref, up_ref, after_ref, gate_out_ref, up_out_ref):
    gate = gate_ref[0].astype(jnp.float32)
    up = up_ref[0].astype(jnp.float32)
    grad = grad_ref[0].astype(jnp.float32)
    sigmoid_gate = jax.nn.sigmoid(gate)
    gate_out_ref[0] = (grad * up * sigmoid_gate * (1.0 + gate * (1.0 - sigmoid_gate))).astype(jnp.bfloat16)
    up_out_ref[0] = (grad * (gate * sigmoid_gate)).astype(jnp.bfloat16)


def gate_up_grads(own_grad, gate_pre, up_pre, after):
    experts, rows, width = gate_pre.shape
    block = pl.BlockSpec((1, rows, width), lambda i: (i, 0, 0))
    return pl.pallas_call(
        gate_up_kernel,
        grid=(experts,),
        in_specs=[block, block, block, pl.BlockSpec(memory_space=pl.ANY)],
        out_specs=[block, block],
        out_shape=[jax.ShapeDtypeStruct(gate_pre.shape, jnp.bfloat16)] * 2,
        name="gate_up_grads",
    )(own_grad, gate_pre, up_pre, after)


def dispatch_kernel(first_ref, rows_ref, weight_ref, after_ref, placed_ref, partial_ref):
    blocks, halves, padded, _ = rows_ref.shape
    experts_here = weight_ref.shape[0]
    half = padded - META
    tokens = halves * half
    before = lax.broadcasted_iota(jnp.int32, (tokens, tokens), 0)
    after = lax.broadcasted_iota(jnp.int32, (tokens, tokens), 1)
    earlier = (before < after).astype(jnp.bfloat16)
    slot_row = lax.broadcasted_iota(jnp.int32, (CAP, tokens), 0).astype(jnp.float32)
    first = first_ref[0].astype(jnp.float32)
    for block in range(blocks):
        meta = rows_ref[block, 0, half:padded, 0:tokens].astype(jnp.float32)
        first_id, second_id = meta[0:1], meta[1:2]
        first_prob = (meta[2:3] + meta[3:4]) + meta[4:5]
        second_prob = (meta[5:6] + meta[6:7]) + meta[7:8]
        members, probs = [], []
        for expert in range(experts_here):
            one = first_id == first + expert
            two = second_id == first + expert
            members.append(jnp.logical_or(one, two).astype(jnp.float32))
            probs.append(jnp.where(one, first_prob, jnp.where(two, second_prob, 0.0)))
        member = jnp.concatenate(members + [jnp.zeros((8 - experts_here, tokens), jnp.float32)], axis=0)
        slots = jnp.dot(member.astype(jnp.bfloat16), earlier, preferred_element_type=jnp.float32)
        tokens_here = jnp.concatenate([rows_ref[block, part, 0:half, :] for part in range(halves)], axis=0)
        for expert in range(experts_here):
            chosen = jnp.where(slot_row == slots[expert : expert + 1], members[expert], 0.0)
            scale = jnp.sum(chosen * probs[expert], axis=1, keepdims=True)
            picked = jnp.dot(chosen.astype(jnp.bfloat16), tokens_here, preferred_element_type=jnp.float32)
            placed_ref[expert, block * CAP : (block + 1) * CAP, :] = (picked * scale).astype(jnp.bfloat16)
    for expert in range(experts_here):
        partial_ref[expert] = lax.dot_general(
            placed_ref[expert],
            weight_ref[expert],
            (((1,), (1,)), ((), ())),
            preferred_element_type=jnp.float32,
        ).astype(jnp.bfloat16)


def dispatch_and_project(first_expert, gathered, down_weight, after, owners):
    sources, halves, padded, width = gathered.shape
    experts_here, hidden_width, _ = down_weight.shape
    rows = sources * CAP
    per_step = sources // owners
    return pl.pallas_call(
        dispatch_kernel,
        grid_spec=pltpu.PrefetchScalarGridSpec(
            num_scalar_prefetch=1,
            grid=(owners,),
            in_specs=[
                pl.BlockSpec((per_step, halves, padded, width), lambda i, s: (i, 0, 0, 0)),
                pl.BlockSpec((experts_here, hidden_width, width), lambda i, s: (0, 0, 0)),
                pl.BlockSpec(memory_space=pl.ANY),
            ],
            out_specs=[
                pl.BlockSpec((experts_here, per_step * CAP, width), lambda i, s: (0, i, 0)),
                pl.BlockSpec((experts_here, per_step * CAP, hidden_width), lambda i, s: (0, i, 0)),
            ],
        ),
        out_shape=[
            jax.ShapeDtypeStruct((experts_here, rows, width), jnp.bfloat16),
            jax.ShapeDtypeStruct((experts_here, rows, hidden_width), jnp.bfloat16),
        ],
        compiler_params=pltpu.CompilerParams(dimension_semantics=("arbitrary",)),
        name="dispatch_project",
    )(first_expert.reshape(1), gathered, down_weight, after)


def three_pieces(value):
    high = lax.reduce_precision(value, 8, 7)
    rest = value - high
    middle = lax.reduce_precision(rest, 8, 7)
    return high, middle, rest - middle


def total_over_mesh(value):
    row = jnp.full((1, 128), value, jnp.float32)
    for axis in ("dp", "ffn", "expert"):
        size = lax.axis_size(axis)
        copies = jnp.broadcast_to(row, (size, 128))
        if size == 2:
            row = row + lax.ppermute(row, axis, [(0, 1), (1, 0)])
        else:
            row = jnp.sum(lax.all_to_all(copies, axis, 0, 0, tiled=True), axis=0, keepdims=True)
    return row[0, 0]


def on_device(grad_rows, gate_probs, expert_ids, gate_pre, up_pre, down_weight):
    experts_here, rows_here, hidden_width = gate_pre.shape
    tokens_here, feature_width = grad_rows.shape
    cores = lax.axis_size("expert")
    sources = lax.axis_size("dp")
    owners = lax.axis_size("ffn")
    experts_total = experts_here * cores
    core = lax.axis_index("expert")
    half = tokens_here // cores

    pieces = [expert_ids[:, 0].astype(jnp.float32), expert_ids[:, 1].astype(jnp.float32)]
    pieces += list(three_pieces(gate_probs[:, 0])) + list(three_pieces(gate_probs[:, 1]))
    meta = jnp.stack(pieces).astype(jnp.bfloat16)
    meta = jnp.pad(meta, ((0, 0), (0, feature_width - tokens_here)))
    own_rows = lax.dynamic_slice_in_dim(grad_rows, core * half, half, axis=0)
    payload = jnp.concatenate([own_rows, meta], axis=0)
    gathered = lax.all_gather(payload, ("dp", "expert"), axis=0, tiled=False)
    gathered = gathered.reshape(sources, cores, half + META, feature_width)

    spread = hidden_copies(gate_pre, up_pre, owners)
    hidden_all = lax.all_to_all(spread, "ffn", 0, 0, tiled=True)

    arrived, partial_sums = dispatch_and_project(
        core * experts_here, gathered, down_weight, hidden_all, owners
    )
    own_grad = lax.psum_scatter(partial_sums, "ffn", scatter_dimension=1, tiled=True)

    weight_grad = jnp.einsum(
        "zerf,ezrd->efd",
        hidden_all,
        arrived.reshape(experts_here, owners, rows_here, feature_width),
        preferred_element_type=jnp.float32,
    )
    squares = total_over_mesh(jnp.sum(weight_grad * weight_grad))
    entry_count = (
        float(experts_total) * float(hidden_width * sources) * float(feature_width * owners)
    )
    clip_limit = jnp.float32(0.5 * math.sqrt(entry_count))
    factor = clip_limit / jnp.maximum(jnp.sqrt(squares), clip_limit)
    down_grad = (weight_grad * factor).astype(jnp.bfloat16)

    gate_grad, up_grad = gate_up_grads(own_grad, gate_pre, up_pre, down_grad)
    return (down_grad, gate_grad, up_grad)


def solution(mesh):
    placed = (
        P("dp", "ffn"),
        P("dp", None),
        P("dp", None),
        P("expert", "ffn", "dp"),
        P("expert", "ffn", "dp"),
        P("expert", "dp", "ffn"),
    )
    return jax.shard_map(
        on_device,
        mesh=mesh,
        in_specs=placed,
        out_specs=(P("expert", "dp", "ffn"), P("expert", "ffn", "dp"), P("expert", "ffn", "dp")),
        check_vma=False,
    )
```

```python
import math

import jax
import jax.numpy as jnp
from jax import lax
from jax.experimental import pallas as pl
from jax.experimental.pallas import tpu as pltpu
from jax.sharding import Mesh
from jax.sharding import PartitionSpec as P

CAP = 72
META = 8
X_CHIPS = 4


def hidden_kernel(gate_ref, up_ref, hidden_ref):
    gate = gate_ref[...].astype(jnp.float32)
    up = up_ref[...].astype(jnp.float32)
    hidden_ref[...] = (gate * jax.nn.sigmoid(gate) * up).astype(jnp.bfloat16)


def hidden_rows(gate_pre, up_pre):
    experts, rows, width = gate_pre.shape
    block = pl.BlockSpec((1, rows, width), lambda i: (i, 0, 0))
    return pl.pallas_call(
        hidden_kernel,
        grid=(experts,),
        in_specs=[block, block],
        out_specs=block,
        out_shape=jax.ShapeDtypeStruct(gate_pre.shape, jnp.bfloat16),
        name="hidden_rows",
    )(gate_pre, up_pre)


def gate_up_kernel(grad_ref, gate_ref, up_ref, after_ref, gate_out_ref, up_out_ref):
    gate = gate_ref[0].astype(jnp.float32)
    up = up_ref[0].astype(jnp.float32)
    grad = grad_ref[0].astype(jnp.float32)
    sigmoid_gate = jax.nn.sigmoid(gate)
    gate_out_ref[0] = (grad * up * sigmoid_gate * (1.0 + gate * (1.0 - sigmoid_gate))).astype(jnp.bfloat16)
    up_out_ref[0] = (grad * (gate * sigmoid_gate)).astype(jnp.bfloat16)


def gate_up_grads(own_grad, gate_pre, up_pre, after):
    experts, rows, width = gate_pre.shape
    block = pl.BlockSpec((1, rows, width), lambda i: (i, 0, 0))
    return pl.pallas_call(
        gate_up_kernel,
        grid=(experts,),
        in_specs=[block, block, block, pl.BlockSpec(memory_space=pl.ANY)],
        out_specs=[block, block],
        out_shape=[jax.ShapeDtypeStruct(gate_pre.shape, jnp.bfloat16)] * 2,
        name="gate_up_grads",
    )(own_grad, gate_pre, up_pre, after)


def dispatch_kernel(place_ref, own_ref, other_ref, weight_ref, *refs):
    placed_ref, partial_ref = refs[-2:]
    blocks, padded, _ = own_ref.shape
    experts_here = weight_ref.shape[0]
    half = padded - META
    tokens = 2 * half
    before = lax.broadcasted_iota(jnp.int32, (tokens, tokens), 0)
    after = lax.broadcasted_iota(jnp.int32, (tokens, tokens), 1)
    earlier = (before < after).astype(jnp.bfloat16)
    slot_row = lax.broadcasted_iota(jnp.int32, (CAP, tokens), 0).astype(jnp.float32)
    core = place_ref[1]
    first = (core * experts_here).astype(jnp.float32)
    for block in range(blocks):
        meta = own_ref[block, half:padded, 0:tokens].astype(jnp.float32)
        first_id, second_id = meta[0:1], meta[1:2]
        first_prob = (meta[2:3] + meta[3:4]) + meta[4:5]
        second_prob = (meta[5:6] + meta[6:7]) + meta[7:8]
        members, probs = [], []
        for expert in range(experts_here):
            one = first_id == first + expert
            two = second_id == first + expert
            members.append(jnp.logical_or(one, two).astype(jnp.float32))
            probs.append(jnp.where(one, first_prob, jnp.where(two, second_prob, 0.0)))
        filler = [jnp.zeros((8 - experts_here, tokens), jnp.float32)]
        member = jnp.concatenate(members + filler, axis=0)
        slots = jnp.dot(member.astype(jnp.bfloat16), earlier, preferred_element_type=jnp.float32)
        slots = jnp.where(member > 0.0, slots, -1.0)
        prob = jnp.concatenate(probs + filler, axis=0)
        slots = jnp.where(core == 1, pltpu.roll(slots, half, 1), slots)
        prob = jnp.where(core == 1, pltpu.roll(prob, half, 1), prob)
        tokens_here = jnp.concatenate([own_ref[block, 0:half, :], other_ref[block, 0:half, :]], axis=0)
        chosen, scales = [], []
        for expert in range(experts_here):
            match = (slot_row == slots[expert : expert + 1]).astype(jnp.float32)
            chosen.append(match)
            scales.append(jnp.sum(match * prob[expert : expert + 1], axis=1, keepdims=True))
        picked = jnp.dot(
            jnp.concatenate(chosen, axis=0).astype(jnp.bfloat16),
            tokens_here,
            preferred_element_type=jnp.float32,
        )
        scaled = (picked * jnp.concatenate(scales, axis=0)).astype(jnp.bfloat16)
        for expert in range(experts_here):
            placed_ref[expert, block * CAP : (block + 1) * CAP, :] = scaled[expert * CAP : (expert + 1) * CAP]
    for expert in range(experts_here):
        partial_ref[expert] = lax.dot_general(
            placed_ref[expert],
            weight_ref[expert],
            (((1,), (1,)), ((), ())),
            preferred_element_type=jnp.float32,
        ).astype(jnp.bfloat16)


def dispatch_and_project(plane, core, own_half, other_half, down_weight, rows, buffers):
    sources, padded, width = own_half.shape
    experts_here, hidden_width, _ = down_weight.shape
    steps = 2
    per_step = sources // steps
    half_block = pl.BlockSpec((per_step, padded, width), lambda i, s: (i, 0, 0))
    anywhere = [pl.BlockSpec(memory_space=pl.ANY)] * len(buffers)
    return pl.pallas_call(
        dispatch_kernel,
        grid_spec=pltpu.PrefetchScalarGridSpec(
            num_scalar_prefetch=1,
            grid=(steps,),
            in_specs=[
                half_block,
                half_block,
                pl.BlockSpec((experts_here, hidden_width, width), lambda i, s: (0, 0, 0)),
            ]
            + anywhere,
            out_specs=[
                pl.BlockSpec((experts_here, per_step * CAP, width), lambda i, s: (0, s[0] * steps + i, 0)),
                pl.BlockSpec((experts_here, per_step * CAP, hidden_width), lambda i, s: (0, s[0] * steps + i, 0)),
            ],
        ),
        out_shape=[
            jax.ShapeDtypeStruct((experts_here, rows, width), jnp.bfloat16),
            jax.ShapeDtypeStruct((experts_here, rows, hidden_width), jnp.bfloat16),
        ],
        input_output_aliases={4 + i: i for i in range(len(buffers))},
        compiler_params=pltpu.CompilerParams(dimension_semantics=("arbitrary",)),
        name="dispatch_project",
    )(jnp.stack([plane, core]).astype(jnp.int32), own_half, other_half, down_weight, *buffers)


def three_pieces(value):
    high = lax.reduce_precision(value, 8, 7)
    rest = value - high
    middle = lax.reduce_precision(rest, 8, 7)
    return high, middle, rest - middle


def total_over_mesh(value):
    row = jnp.full((1, 128), value, jnp.float32)
    for axis in (("x", "y"), "ffn"):
        copies = jnp.broadcast_to(row, (lax.axis_size(axis), 128))
        row = jnp.sum(lax.all_to_all(copies, axis, 0, 0, tiled=True), axis=0, keepdims=True)
    row = row + swap_cores(row)
    return row[0, 0]


def swap_cores(value):
    return lax.ppermute(value, "expert", [(0, 1), (1, 0)])


def along_x(value):
    size = lax.axis_size("x")
    pairs = []
    for place in range(size):
        pairs.append((place * 2, (place + 1) % size * 2))
        pairs.append((place * 2 + 1, (place - 1) % size * 2 + 1))
    return lax.ppermute(value, ("x", "expert"), pairs)


def on_device(grad_rows, gate_probs, expert_ids, gate_pre, up_pre, down_weight):
    experts_here, rows_here, hidden_width = gate_pre.shape
    tokens_here, feature_width = grad_rows.shape
    cores = lax.axis_size("expert")
    planes = lax.axis_size("x")
    lines = lax.axis_size("y")
    sources = planes * lines
    owners = lax.axis_size("ffn")
    experts_total = experts_here * cores
    core = lax.axis_index("expert")
    plane = lax.axis_index("x")
    half = tokens_here // cores
    rows = rows_here * owners

    pieces = [expert_ids[:, 0].astype(jnp.float32), expert_ids[:, 1].astype(jnp.float32)]
    pieces += list(three_pieces(gate_probs[:, 0])) + list(three_pieces(gate_probs[:, 1]))
    meta = jnp.stack(pieces).astype(jnp.bfloat16)
    meta = jnp.pad(meta, ((0, 0), (0, feature_width - tokens_here)))
    own_rows = lax.dynamic_slice_in_dim(grad_rows, core * half, half, axis=0)
    payload = jnp.concatenate([own_rows, meta], axis=0)
    near = lax.all_to_all(
        jnp.broadcast_to(payload[None], (lines,) + payload.shape), "y", 0, 0, tiled=True
    )

    hidden_all = lax.all_gather(hidden_rows(gate_pre, up_pre), "ffn", axis=1, tiled=True)

    side_own = along_x(near)
    near_other = swap_cores(near)
    side_other = along_x(near_other)
    far_own = along_x(side_own)
    beyond_other = swap_cores(side_own)
    beyond_own = swap_cores(side_other)

    def project(offset, own_half, other_half, buffers):
        return dispatch_and_project(
            (plane + offset) % planes, core, own_half, other_half, down_weight, rows, buffers
        )

    buffers = project(0, near, near_other, ())
    buffers = project(planes - 1 + 2 * core, side_own, side_other, buffers)
    far_own, buffers = lax.optimization_barrier((far_own, buffers))
    far_other = swap_cores(far_own)
    buffers = project(1 + planes - 2 * core, beyond_own, beyond_other, buffers)
    buffers = project(2, far_own, far_other, buffers)
    arrived, partial_sums = buffers
    own_grad = lax.psum_scatter(partial_sums, "ffn", scatter_dimension=1, tiled=True)

    weight_grad = jnp.einsum(
        "erf,erd->efd",
        hidden_all,
        arrived,
        preferred_element_type=jnp.float32,
    )
    squares = total_over_mesh(jnp.sum(weight_grad * weight_grad))
    entry_count = (
        float(experts_total) * float(hidden_width * sources) * float(feature_width * owners)
    )
    clip_limit = jnp.float32(0.5 * math.sqrt(entry_count))
    factor = clip_limit / jnp.maximum(jnp.sqrt(squares), clip_limit)
    down_grad = (weight_grad * factor).astype(jnp.bfloat16)

    gate_grad, up_grad = gate_up_grads(own_grad, gate_pre, up_pre, down_grad)
    return (down_grad, gate_grad, up_grad)


def solution(mesh):
    fine = Mesh(mesh.devices.reshape((X_CHIPS, -1) + mesh.devices.shape[1:]), ("x", "y", "expert", "ffn"))
    spread = ("x", "y")
    placed = (
        P(spread, "ffn"),
        P(spread, None),
        P(spread, None),
        P("expert", "ffn", spread),
        P("expert", "ffn", spread),
        P("expert", spread, "ffn"),
    )
    return jax.shard_map(
        on_device,
        mesh=fine,
        in_specs=placed,
        out_specs=(P("expert", spread, "ffn"), P("expert", "ffn", spread), P("expert", "ffn", spread)),
        check_vma=False,
    )
```

```python
import math

import jax
import jax.numpy as jnp
from jax import lax
from jax.experimental import pallas as pl
from jax.experimental.pallas import tpu as pltpu
from jax.sharding import Mesh
from jax.sharding import PartitionSpec as P

CAP = 72
META = 8
LANES = 128
X_CHIPS = 4
VMEM_GRANT = 16 * 2**20


def prepare_kernel(core_ref, rows_ref, ids_ref, probs_ref, gate_ref, up_ref, payload_ref, hidden_ref):
    lanes = payload_ref.shape[2]
    half = rows_ref.shape[0] // 2
    rows = rows_ref[pl.ds(core_ref[0] * half, half), :]
    probs = probs_ref[...]
    high = probs.astype(jnp.bfloat16).astype(jnp.float32)
    middle = (probs - high).astype(jnp.bfloat16).astype(jnp.float32)
    low = (probs - high) - middle
    lines = [ids_ref[...].astype(jnp.float32)]
    for route in range(probs.shape[0]):
        lines += [piece[route : route + 1] for piece in (high, middle, low)]
    meta = jnp.concatenate(lines, axis=0).astype(jnp.bfloat16)
    strips = [rows[:, start : start + lanes] for start in range(0, rows.shape[1], lanes)]
    payload = jnp.concatenate(strips + [meta], axis=0)
    for copy in range(payload_ref.shape[0]):
        payload_ref[copy] = payload
    gate = gate_ref[...].astype(jnp.float32)
    up = up_ref[...].astype(jnp.float32)
    hidden_ref[...] = (gate * jax.nn.sigmoid(gate) * up).astype(jnp.bfloat16)


def prepare(core, grad_rows, expert_ids, gate_probs, gate_pre, up_pre, copies):
    tokens, width = grad_rows.shape
    padded = tokens * width // (2 * LANES) + META
    operands = (grad_rows, expert_ids.T, gate_probs.T, gate_pre, up_pre)
    results = [
        jax.ShapeDtypeStruct((copies, padded, LANES), jnp.bfloat16),
        jax.ShapeDtypeStruct(gate_pre.shape, jnp.bfloat16),
    ]

    def whole(array):
        zeros = (0,) * len(array.shape)
        return pl.BlockSpec(array.shape, lambda i: zeros)

    return pl.pallas_call(
        prepare_kernel,
        grid=(1,),
        in_specs=[pl.BlockSpec(memory_space=pltpu.SMEM)] + [whole(operand) for operand in operands],
        out_specs=[whole(result) for result in results],
        out_shape=results,
        name="prepare",
    )(core.reshape(1), *operands)


def gate_up_kernel(grad_ref, gate_ref, up_ref, after_ref, gate_out_ref, up_out_ref):
    gate = gate_ref[0].astype(jnp.float32)
    up = up_ref[0].astype(jnp.float32)
    grad = grad_ref[0].astype(jnp.float32)
    sigmoid_gate = jax.nn.sigmoid(gate)
    gate_out_ref[0] = (grad * up * sigmoid_gate * (1.0 + gate * (1.0 - sigmoid_gate))).astype(jnp.bfloat16)
    up_out_ref[0] = (grad * (gate * sigmoid_gate)).astype(jnp.bfloat16)


def gate_up_grads(own_grad, gate_pre, up_pre, after):
    experts, rows, width = gate_pre.shape
    block = pl.BlockSpec((1, rows, width), lambda i: (i, 0, 0))
    return pl.pallas_call(
        gate_up_kernel,
        grid=(experts,),
        in_specs=[block, block, block, pl.BlockSpec(memory_space=pl.ANY)],
        out_specs=[block, block],
        out_shape=[jax.ShapeDtypeStruct(gate_pre.shape, jnp.bfloat16)] * 2,
        name="gate_up_grads",
    )(own_grad, gate_pre, up_pre, after)


def dispatch_kernel(place_ref, own_ref, other_ref, weight_ref, *refs):
    placed_ref, partial_ref = refs[-2:]
    step = pl.program_id(0)
    meta_start = own_ref.shape[1] - META
    experts_here, width, _ = weight_ref.shape
    half = meta_start * LANES // width
    tokens = 2 * half
    blocks = placed_ref.shape[1] // CAP
    before = lax.broadcasted_iota(jnp.int32, (tokens, tokens), 0)
    after = lax.broadcasted_iota(jnp.int32, (tokens, tokens), 1)
    earlier = (before < after).astype(jnp.bfloat16)
    slot_row = lax.broadcasted_iota(jnp.int32, (CAP, tokens), 0).astype(jnp.float32)
    core = place_ref[4]
    first = (core * experts_here).astype(jnp.float32)
    members, probs = [], []
    for block in range(blocks):
        meta = own_ref[step * blocks + block, meta_start : meta_start + META, :].astype(jnp.float32)
        first_id, second_id = meta[0:1], meta[1:2]
        first_prob = (meta[2:3] + meta[3:4]) + meta[4:5]
        second_prob = (meta[5:6] + meta[6:7]) + meta[7:8]
        for expert in range(experts_here):
            one = first_id == first + expert
            two = second_id == first + expert
            members.append(jnp.logical_or(one, two).astype(jnp.float32))
            probs.append(jnp.where(one, first_prob, jnp.where(two, second_prob, 0.0)))
    member = jnp.concatenate(members, axis=0)
    slots = jnp.dot(member.astype(jnp.bfloat16), earlier, preferred_element_type=jnp.float32)
    slots = jnp.where(member > 0.0, slots, -1.0)
    prob = jnp.concatenate(probs, axis=0)
    slots = jnp.where(core == 1, pltpu.roll(slots, half, 1), slots)
    prob = jnp.where(core == 1, pltpu.roll(prob, half, 1), prob)
    for block in range(blocks):
        index = step * blocks + block
        strips = [
            jnp.concatenate([ref[index, start : start + half, :] for ref in (own_ref, other_ref)], axis=0)
            for start in range(0, meta_start, half)
        ]
        tokens_here = jnp.concatenate(strips, axis=1)
        chosen, scales = [], []
        for expert in range(experts_here):
            line = block * experts_here + expert
            match = (slot_row == slots[line : line + 1]).astype(jnp.float32)
            chosen.append(match)
            scales.append(jnp.sum(match * prob[line : line + 1], axis=1, keepdims=True))
        picked = jnp.dot(
            jnp.concatenate(chosen, axis=0).astype(jnp.bfloat16),
            tokens_here,
            preferred_element_type=jnp.float32,
        )
        scaled = (picked * jnp.concatenate(scales, axis=0)).astype(jnp.bfloat16)
        for expert in range(experts_here):
            placed_ref[expert, block * CAP : (block + 1) * CAP, :] = scaled[expert * CAP : (expert + 1) * CAP]
    for expert in range(experts_here):
        partial_ref[expert] = jnp.dot(
            placed_ref[expert], weight_ref[expert], preferred_element_type=jnp.float32
        ).astype(jnp.bfloat16)


def dispatch_and_project(turn, places, own_half, other_half, weight, rows, owners, buffers):
    experts_here, width, hidden_width = weight.shape
    steps = 2
    per_owner = rows // owners
    resident = pl.BlockSpec(memory_space=pltpu.VMEM)
    anywhere = [pl.BlockSpec(memory_space=pltpu.HBM)] * len(buffers)
    return pl.pallas_call(
        dispatch_kernel,
        grid_spec=pltpu.PrefetchScalarGridSpec(
            num_scalar_prefetch=1,
            grid=(steps,),
            in_specs=[resident, resident, resident] + anywhere,
            out_specs=[
                pl.BlockSpec((experts_here, per_owner, width), lambda i, s: (0, s[turn] * steps + i, 0)),
                pl.BlockSpec((experts_here, per_owner, hidden_width), lambda i, s: (0, s[turn] * steps + i, 0)),
            ],
        ),
        out_shape=[
            pltpu.HBM((experts_here, rows, width), jnp.bfloat16),
            pltpu.HBM((experts_here, rows, hidden_width), jnp.bfloat16),
        ],
        input_output_aliases={4 + i: i for i in range(len(buffers))},
        compiler_params=pltpu.CompilerParams(dimension_semantics=("arbitrary",), vmem_limit_bytes=VMEM_GRANT),
        name="dispatch_project",
    )(places, own_half, other_half, weight, *buffers)


def weight_grad_kernel(hidden_ref, placed_ref, grad_ref, squares_ref, total_ref):
    expert = pl.program_id(0)
    grad = lax.dot_general(
        hidden_ref[0], placed_ref[0], (((0,), (0,)), ((), ())), preferred_element_type=jnp.float32
    )
    grad_ref[0] = grad
    squares = jnp.sum(grad * grad, axis=0, keepdims=True)

    @pl.when(expert == 0)
    def _():
        total_ref[...] = squares

    @pl.when(expert > 0)
    def _():
        total_ref[...] += squares

    @pl.when(expert == pl.num_programs(0) - 1)
    def _():
        squares_ref[...] = jnp.full(squares_ref.shape, jnp.sum(total_ref[...]), jnp.float32)


def weight_grads(hidden_all, arrived, copies):
    experts, rows, hidden_width = hidden_all.shape
    width = arrived.shape[2]
    return pl.pallas_call(
        weight_grad_kernel,
        grid=(experts,),
        in_specs=[
            pl.BlockSpec((1, rows, hidden_width), lambda i: (i, 0, 0)),
            pl.BlockSpec((1, rows, width), lambda i: (i, 0, 0)),
        ],
        out_specs=[
            pl.BlockSpec((1, hidden_width, width), lambda i: (i, 0, 0)),
            pl.BlockSpec((copies, 1, LANES), lambda i: (0, 0, 0)),
        ],
        out_shape=[
            jax.ShapeDtypeStruct((experts, hidden_width, width), jnp.float32),
            jax.ShapeDtypeStruct((copies, 1, LANES), jnp.float32),
        ],
        scratch_shapes=[pltpu.VMEM((1, width), jnp.float32)],
        compiler_params=pltpu.CompilerParams(dimension_semantics=("arbitrary",)),
        name="weight_grads",
    )(hidden_all, arrived)


def exchange(value, axis):
    return lax.all_to_all(value, axis, 0, 0, tiled=True)


def to_all(value, axis):
    return exchange(jnp.broadcast_to(value[None], (lax.axis_size(axis),) + value.shape), axis)


def swap_cores(value):
    return lax.ppermute(value, "expert", [(0, 1), (1, 0)])


def along_x(value):
    size = lax.axis_size("x")
    pairs = []
    for place in range(size):
        pairs.append((place * 2, (place + 1) % size * 2))
        pairs.append((place * 2 + 1, (place - 1) % size * 2 + 1))
    return lax.ppermute(value, ("x", "expert"), pairs)


def on_device(grad_rows, gate_probs, expert_ids, gate_pre, up_pre, down_weight):
    experts_here, rows_here, hidden_width = gate_pre.shape
    tokens_here, feature_width = grad_rows.shape
    cores = lax.axis_size("expert")
    planes = lax.axis_size("x")
    lines = lax.axis_size("y")
    sources = planes * lines
    owners = lax.axis_size("ffn")
    experts_total = experts_here * cores
    core = lax.axis_index("expert")
    plane = lax.axis_index("x")
    rows = rows_here * owners

    payload, hidden = prepare(core, grad_rows, expert_ids, gate_probs, gate_pre, up_pre, lines)
    near = exchange(payload, "y")
    hidden_all = lax.all_gather(hidden, "ffn", axis=1, tiled=True)
    weight = jnp.swapaxes(down_weight, 1, 2)
    offsets = [0, planes - 1 + 2 * core, 1 + planes - 2 * core, 2]
    places = jnp.stack([(plane + offset) % planes for offset in offsets] + [core]).astype(jnp.int32)

    def project(turn, own_half, other_half, buffers):
        return dispatch_and_project(
            turn, places, own_half, other_half, weight, rows, owners, buffers
        )

    side_own = along_x(near)
    near_other = swap_cores(near)
    side_other = along_x(near_other)
    buffers = project(0, near, near_other, ())
    side_own, buffers = lax.optimization_barrier((side_own, buffers))
    far_own = along_x(side_own)
    beyond_other = swap_cores(side_own)
    beyond_own = swap_cores(side_other)
    buffers = project(1, side_own, side_other, buffers)
    far_own, buffers = lax.optimization_barrier((far_own, buffers))
    far_other = swap_cores(far_own)
    buffers = project(2, beyond_own, beyond_other, buffers)
    arrived, partial_terms = project(3, far_own, far_other, buffers)
    own_grad = lax.psum_scatter(partial_terms, "ffn", scatter_dimension=1, tiled=True)

    weight_grad, squares = weight_grads(hidden_all, arrived, sources)
    squares = jnp.sum(exchange(squares, ("x", "y")), axis=0)
    squares = jnp.sum(to_all(squares, ("expert", "ffn"))[:, 0, 0])
    entry_count = (
        float(experts_total) * float(hidden_width * sources) * float(feature_width * owners)
    )
    clip_limit = jnp.float32(0.5 * math.sqrt(entry_count))
    factor = clip_limit / jnp.maximum(jnp.sqrt(squares), clip_limit)
    down_grad = (weight_grad * factor).astype(jnp.bfloat16)

    gate_grad, up_grad = gate_up_grads(own_grad, gate_pre, up_pre, down_grad)
    return (down_grad, gate_grad, up_grad)


def solution(mesh):
    fine = Mesh(mesh.devices.reshape((X_CHIPS, -1) + mesh.devices.shape[1:]), ("x", "y", "expert", "ffn"))
    spread = ("x", "y")
    placed = (
        P(spread, "ffn"),
        P(spread, None),
        P(spread, None),
        P("expert", "ffn", spread),
        P("expert", "ffn", spread),
        P("expert", spread, "ffn"),
    )
    return jax.shard_map(
        on_device,
        mesh=fine,
        in_specs=placed,
        out_specs=(P("expert", spread, "ffn"), P("expert", "ffn", spread), P("expert", "ffn", spread)),
        check_vma=False,
    )
```

```python
import functools
import math

import jax
import jax.numpy as jnp
from jax import lax
from jax.experimental import pallas as pl
from jax.experimental.pallas import tpu as pltpu
from jax.sharding import Mesh
from jax.sharding import PartitionSpec as P

CAP = 72
META = 8
LANES = 128
X_CHIPS = 4
VMEM_GRANT = 16 * 2**20


def prepare_kernel(core_ref, rows_ref, ids_ref, probs_ref, gate_ref, up_ref, payload_ref, hidden_ref):
    lanes = payload_ref.shape[2]
    half = rows_ref.shape[0] // 2
    rows = rows_ref[pl.ds(core_ref[0] * half, half), :]
    probs = probs_ref[...]
    high = probs.astype(jnp.bfloat16).astype(jnp.float32)
    middle = (probs - high).astype(jnp.bfloat16).astype(jnp.float32)
    low = (probs - high) - middle
    lines = [ids_ref[...].astype(jnp.float32)]
    for route in range(probs.shape[0]):
        lines += [piece[route : route + 1] for piece in (high, middle, low)]
    meta = jnp.concatenate(lines, axis=0).astype(jnp.bfloat16)
    strips = [rows[:, start : start + lanes] for start in range(0, rows.shape[1], lanes)]
    payload = jnp.concatenate(strips + [meta], axis=0)
    for copy in range(payload_ref.shape[0]):
        payload_ref[copy] = payload
    gate = gate_ref[...].astype(jnp.float32)
    up = up_ref[...].astype(jnp.float32)
    hidden_ref[...] = (gate * jax.nn.sigmoid(gate) * up).astype(jnp.bfloat16)


def prepare(core, grad_rows, expert_ids, gate_probs, gate_pre, up_pre, copies):
    tokens, width = grad_rows.shape
    padded = tokens * width // (2 * LANES) + META
    operands = (grad_rows, expert_ids.T, gate_probs.T, gate_pre, up_pre)
    results = [
        jax.ShapeDtypeStruct((copies, padded, LANES), jnp.bfloat16),
        jax.ShapeDtypeStruct(gate_pre.shape, jnp.bfloat16),
    ]

    def whole(array):
        zeros = (0,) * len(array.shape)
        return pl.BlockSpec(array.shape, lambda i: zeros)

    return pl.pallas_call(
        prepare_kernel,
        grid=(1,),
        in_specs=[pl.BlockSpec(memory_space=pltpu.SMEM)] + [whole(operand) for operand in operands],
        out_specs=[whole(result) for result in results],
        out_shape=results,
        name="prepare",
    )(core.reshape(1), *operands)


def gate_up_kernel(grad_ref, gate_ref, up_ref, after_ref, gate_out_ref, up_out_ref):
    gate = gate_ref[0].astype(jnp.float32)
    up = up_ref[0].astype(jnp.float32)
    grad = grad_ref[0].astype(jnp.float32)
    sigmoid_gate = jax.nn.sigmoid(gate)
    gate_out_ref[0] = (grad * up * sigmoid_gate * (1.0 + gate * (1.0 - sigmoid_gate))).astype(jnp.bfloat16)
    up_out_ref[0] = (grad * (gate * sigmoid_gate)).astype(jnp.bfloat16)


def gate_up_grads(own_grad, gate_pre, up_pre, after):
    experts, rows, width = gate_pre.shape
    block = pl.BlockSpec((1, rows, width), lambda i: (i, 0, 0))
    return pl.pallas_call(
        gate_up_kernel,
        grid=(experts,),
        in_specs=[block, block, block, pl.BlockSpec(memory_space=pl.ANY)],
        out_specs=[block, block],
        out_shape=[pltpu.HBM(gate_pre.shape, jnp.bfloat16)] * 2,
        compiler_params=pltpu.CompilerParams(vmem_limit_bytes=VMEM_GRANT),
        name="gate_up_grads",
    )(pltpu.with_memory_space_constraint(own_grad, pltpu.HBM), gate_pre, up_pre, after)


def dispatch_kernel(turn, place_ref, own_ref, other_ref, weight_ref, *refs):
    placed_out, partial_out, placed_ref, partial_ref, placed_sems, partial_sems = refs[-6:]
    sources = own_ref.shape[0]
    meta_start = own_ref.shape[1] - META
    experts_here, width, _ = weight_ref.shape
    half = meta_start * LANES // width
    tokens = 2 * half
    steps = partial_ref.shape[0]
    blocks = sources // steps
    before = lax.broadcasted_iota(jnp.int32, (tokens, tokens), 0)
    after = lax.broadcasted_iota(jnp.int32, (tokens, tokens), 1)
    earlier = (before < after).astype(jnp.bfloat16)
    slot_row = lax.broadcasted_iota(jnp.int32, (CAP, tokens), 0).astype(jnp.float32)
    plane = place_ref[turn]
    core = place_ref[4]
    first = (core * experts_here).astype(jnp.float32)
    members, probs = [], []
    for block in range(sources):
        meta = own_ref[block, meta_start : meta_start + META, :].astype(jnp.float32)
        first_id, second_id = meta[0:1], meta[1:2]
        first_prob = (meta[2:3] + meta[3:4]) + meta[4:5]
        second_prob = (meta[5:6] + meta[6:7]) + meta[7:8]
        for expert in range(experts_here):
            one = first_id == first + expert
            two = second_id == first + expert
            members.append(jnp.logical_or(one, two).astype(jnp.float32))
            probs.append(jnp.where(one, first_prob, jnp.where(two, second_prob, 0.0)))
    member = jnp.concatenate(members, axis=0)
    slots = jnp.dot(member.astype(jnp.bfloat16), earlier, preferred_element_type=jnp.float32)
    slots = jnp.where(member > 0.0, slots, -1.0)
    prob = jnp.concatenate(probs, axis=0)
    slots = jnp.where(core == 1, pltpu.roll(slots, half, 1), slots)
    prob = jnp.where(core == 1, pltpu.roll(prob, half, 1), prob)
    copies = []
    for block in range(sources):
        strips = [
            jnp.concatenate([ref[block, start : start + half, :] for ref in (own_ref, other_ref)], axis=0)
            for start in range(0, meta_start, half)
        ]
        tokens_here = jnp.concatenate(strips, axis=1)
        chosen, scales = [], []
        for expert in range(experts_here):
            line = block * experts_here + expert
            match = (slot_row == slots[line : line + 1]).astype(jnp.float32)
            chosen.append(match)
            scales.append(jnp.sum(match * prob[line : line + 1], axis=1, keepdims=True))
        picked = jnp.dot(
            jnp.concatenate(chosen, axis=0).astype(jnp.bfloat16),
            tokens_here,
            preferred_element_type=jnp.float32,
        )
        scaled = (picked * jnp.concatenate(scales, axis=0)).astype(jnp.bfloat16)
        for expert in range(experts_here):
            placed_ref[expert, block * CAP : (block + 1) * CAP, :] = scaled[expert * CAP : (expert + 1) * CAP]
        if block % 2 == 1:
            start = (block - 1) * CAP
            target = pl.multiple_of(plane * (sources * CAP) + start, 2 * CAP)
            for expert in range(experts_here):
                copies.append(
                    pltpu.make_async_copy(
                        placed_ref.at[expert, pl.ds(start, 2 * CAP), :],
                        placed_out.at[expert, pl.ds(target, 2 * CAP), :],
                        placed_sems.at[block // 2, expert],
                    )
                )
                copies[-1].start()
        if block % blocks == blocks - 1:
            step = block // blocks
            for expert in range(experts_here):
                partial_ref[step, expert] = jnp.dot(
                    placed_ref[expert, step * blocks * CAP : (step + 1) * blocks * CAP, :],
                    weight_ref[expert],
                    preferred_element_type=jnp.float32,
                ).astype(jnp.bfloat16)
                copies.append(
                    pltpu.make_async_copy(
                        partial_ref.at[step, expert],
                        partial_out.at[plane * steps + step, expert],
                        partial_sems.at[step, expert],
                    )
                )
                copies[-1].start()
    for copy in copies:
        copy.wait()


def dispatch_and_project(turn, places, own_half, other_half, weight, rows, owners, buffers):
    experts_here, width, hidden_width = weight.shape
    sources = own_half.shape[0]
    steps = 2
    per_owner = rows // owners
    resident = pl.BlockSpec(memory_space=pltpu.VMEM)
    outside = pl.BlockSpec(memory_space=pltpu.HBM)
    return pl.pallas_call(
        functools.partial(dispatch_kernel, turn),
        in_specs=[pl.BlockSpec(memory_space=pltpu.SMEM), resident, resident, resident]
        + [outside] * len(buffers),
        out_specs=[outside, outside],
        out_shape=[
            pltpu.HBM((experts_here, rows, width), jnp.bfloat16),
            pltpu.HBM((owners, experts_here, per_owner, hidden_width), jnp.bfloat16),
        ],
        scratch_shapes=[
            pltpu.VMEM((experts_here, steps * per_owner, width), jnp.bfloat16),
            pltpu.VMEM((steps, experts_here, per_owner, hidden_width), jnp.bfloat16),
            pltpu.SemaphoreType.DMA((sources // 2, experts_here)),
            pltpu.SemaphoreType.DMA((steps, experts_here)),
        ],
        input_output_aliases={4 + i: i for i in range(len(buffers))},
        compiler_params=pltpu.CompilerParams(vmem_limit_bytes=VMEM_GRANT),
        name="dispatch_project",
    )(places, own_half, other_half, weight, *buffers)


def weight_grad_kernel(hidden_ref, placed_ref, grad_ref, squares_ref, total_ref):
    expert = pl.program_id(0)
    grad = lax.dot_general(
        hidden_ref[0], placed_ref[0], (((0,), (0,)), ((), ())), preferred_element_type=jnp.float32
    )
    grad_ref[0] = grad
    squares = jnp.sum(grad * grad, axis=0, keepdims=True)

    @pl.when(expert == 0)
    def _():
        total_ref[...] = squares

    @pl.when(expert > 0)
    def _():
        total_ref[...] += squares

    @pl.when(expert == pl.num_programs(0) - 1)
    def _():
        squares_ref[...] = jnp.full(squares_ref.shape, jnp.sum(total_ref[...]), jnp.float32)


def weight_grads(hidden_all, arrived, copies):
    experts, rows, hidden_width = hidden_all.shape
    width = arrived.shape[2]
    return pl.pallas_call(
        weight_grad_kernel,
        grid=(experts,),
        in_specs=[
            pl.BlockSpec((1, rows, hidden_width), lambda i: (i, 0, 0)),
            pl.BlockSpec((1, rows, width), lambda i: (i, 0, 0)),
        ],
        out_specs=[
            pl.BlockSpec((1, hidden_width, width), lambda i: (i, 0, 0)),
            pl.BlockSpec((copies, 1, LANES), lambda i: (0, 0, 0)),
        ],
        out_shape=[
            jax.ShapeDtypeStruct((experts, hidden_width, width), jnp.float32),
            jax.ShapeDtypeStruct((copies, 1, LANES), jnp.float32),
        ],
        scratch_shapes=[pltpu.VMEM((1, width), jnp.float32)],
        compiler_params=pltpu.CompilerParams(
            dimension_semantics=("arbitrary",), vmem_limit_bytes=2 * VMEM_GRANT
        ),
        name="weight_grads",
    )(
        pltpu.with_memory_space_constraint(hidden_all, pltpu.HBM),
        pltpu.with_memory_space_constraint(arrived, pltpu.HBM),
    )


def exchange(value, axis):
    return lax.all_to_all(value, axis, 0, 0, tiled=True)


def to_all(value, axis):
    return exchange(jnp.broadcast_to(value[None], (lax.axis_size(axis),) + value.shape), axis)


def swap_cores(value):
    return lax.ppermute(value, "expert", [(0, 1), (1, 0)])


def along_x(value):
    size = lax.axis_size("x")
    pairs = []
    for place in range(size):
        pairs.append((place * 2, (place + 1) % size * 2))
        pairs.append((place * 2 + 1, (place - 1) % size * 2 + 1))
    return lax.ppermute(value, ("x", "expert"), pairs)


def on_device(grad_rows, gate_probs, expert_ids, gate_pre, up_pre, down_weight):
    experts_here, rows_here, hidden_width = gate_pre.shape
    tokens_here, feature_width = grad_rows.shape
    cores = lax.axis_size("expert")
    planes = lax.axis_size("x")
    lines = lax.axis_size("y")
    sources = planes * lines
    owners = lax.axis_size("ffn")
    experts_total = experts_here * cores
    core = lax.axis_index("expert")
    plane = lax.axis_index("x")
    rows = rows_here * owners

    payload, hidden = prepare(core, grad_rows, expert_ids, gate_probs, gate_pre, up_pre, lines)
    near = exchange(payload, "y")
    hidden_all = lax.all_gather(hidden, "ffn", axis=1, tiled=True)
    weight = jnp.swapaxes(down_weight, 1, 2)
    offsets = [0, planes - 1 + 2 * core, 1 + planes - 2 * core, 2]
    places = jnp.stack([(plane + offset) % planes for offset in offsets] + [core]).astype(jnp.int32)

    def project(turn, own_half, other_half, buffers):
        return dispatch_and_project(
            turn, places, own_half, other_half, weight, rows, owners, buffers
        )

    side_own = along_x(near)
    near_other = swap_cores(near)
    side_other = along_x(near_other)
    buffers = project(0, near, near_other, ())
    side_own, buffers = lax.optimization_barrier((side_own, buffers))
    far_own = along_x(side_own)
    beyond_other = swap_cores(side_own)
    beyond_own = swap_cores(side_other)
    buffers = project(1, side_own, side_other, buffers)
    far_own, buffers = lax.optimization_barrier((far_own, buffers))
    far_other = swap_cores(far_own)
    buffers = project(2, beyond_own, beyond_other, buffers)
    arrived, partial_terms = project(3, far_own, far_other, buffers)
    own_grad = lax.psum_scatter(partial_terms, "ffn", scatter_dimension=0, tiled=True)[0]

    weight_grad, squares = weight_grads(hidden_all, arrived, sources)
    squares = jnp.sum(exchange(squares, ("x", "y")), axis=0)
    squares = jnp.sum(to_all(squares, ("expert", "ffn"))[:, 0, 0])
    entry_count = (
        float(experts_total) * float(hidden_width * sources) * float(feature_width * owners)
    )
    clip_limit = jnp.float32(0.5 * math.sqrt(entry_count))
    factor = clip_limit / jnp.maximum(jnp.sqrt(squares), clip_limit)
    down_grad = (weight_grad * factor).astype(jnp.bfloat16)

    gate_grad, up_grad = gate_up_grads(own_grad, gate_pre, up_pre, down_grad)
    return (down_grad, gate_grad, up_grad)


def solution(mesh):
    fine = Mesh(mesh.devices.reshape((X_CHIPS, -1) + mesh.devices.shape[1:]), ("x", "y", "expert", "ffn"))
    spread = ("x", "y")
    placed = (
        P(spread, "ffn"),
        P(spread, None),
        P(spread, None),
        P("expert", "ffn", spread),
        P("expert", "ffn", spread),
        P("expert", spread, "ffn"),
    )
    return jax.shard_map(
        on_device,
        mesh=fine,
        in_specs=placed,
        out_specs=(P("expert", spread, "ffn"), P("expert", "ffn", spread), P("expert", "ffn", spread)),
        check_vma=False,
    )
```

```python
import functools
import math

import jax
import jax.numpy as jnp
from jax import lax
from jax.experimental import pallas as pl
from jax.experimental.pallas import tpu as pltpu
from jax.sharding import Mesh
from jax.sharding import PartitionSpec as P

CAP = 72
META = 8
LANES = 128
X_CHIPS = 4
VMEM_GRANT = 16 * 2**20


def prepare_kernel(core_ref, rows_ref, ids_ref, probs_ref, gate_ref, up_ref, payload_ref, hidden_ref):
    lanes = payload_ref.shape[2]
    half = rows_ref.shape[0] // 2
    rows = rows_ref[pl.ds(core_ref[0] * half, half), :]
    probs = probs_ref[...]
    high = probs.astype(jnp.bfloat16).astype(jnp.float32)
    middle = (probs - high).astype(jnp.bfloat16).astype(jnp.float32)
    low = (probs - high) - middle
    lines = [ids_ref[...].astype(jnp.float32)]
    for route in range(probs.shape[0]):
        lines += [piece[route : route + 1] for piece in (high, middle, low)]
    meta = jnp.concatenate(lines, axis=0).astype(jnp.bfloat16)
    strips = [rows[:, start : start + lanes] for start in range(0, rows.shape[1], lanes)]
    payload = jnp.concatenate(strips + [meta], axis=0)
    for copy in range(payload_ref.shape[0]):
        payload_ref[copy] = payload
    gate = gate_ref[...].astype(jnp.float32)
    up = up_ref[...].astype(jnp.float32)
    hidden_ref[...] = (gate * jax.nn.sigmoid(gate) * up).astype(jnp.bfloat16)


def prepare(core, grad_rows, expert_ids, gate_probs, gate_pre, up_pre, copies):
    tokens, width = grad_rows.shape
    padded = tokens * width // (2 * LANES) + META
    experts, rows_here, hidden_width = gate_pre.shape
    small = (grad_rows, expert_ids.T, gate_probs.T)
    block = pl.BlockSpec((1, rows_here, hidden_width), lambda i: (i, 0, 0))
    return pl.pallas_call(
        prepare_kernel,
        grid=(experts,),
        in_specs=[pl.BlockSpec(memory_space=pltpu.SMEM)]
        + [pl.BlockSpec(array.shape, lambda i: (0, 0)) for array in small]
        + [block, block],
        out_specs=[pl.BlockSpec((copies // experts, padded, LANES), lambda i: (i, 0, 0)), block],
        out_shape=[
            jax.ShapeDtypeStruct((copies, padded, LANES), jnp.bfloat16),
            jax.ShapeDtypeStruct(gate_pre.shape, jnp.bfloat16),
        ],
        name="prepare",
    )(core.reshape(1), *small, gate_pre, up_pre)


def gate_up_kernel(grad_in, gate_ref, up_ref, after_ref, gate_out, up_out,
                   grad_ref, gate_out_ref, up_out_ref, load_sems, store_sems):
    experts, rows, _ = gate_ref.shape
    parts = load_sems.shape[1]
    size = rows // parts
    spots = [(expert, part) for expert in range(experts) for part in range(parts)]
    loads = []
    for expert, part in spots:
        spot = (expert, pl.ds(part * size, size))
        loads.append(pltpu.make_async_copy(grad_in.at[spot], grad_ref.at[spot], load_sems.at[expert, part]))
        loads[-1].start()
    stores = []
    for load, (expert, part) in zip(loads, spots):
        load.wait()
        spot = (expert, pl.ds(part * size, size))
        gate = gate_ref[spot].astype(jnp.float32)
        up = up_ref[spot].astype(jnp.float32)
        grad = grad_ref[spot].astype(jnp.float32)
        sigmoid_gate = jax.nn.sigmoid(gate)
        slope = sigmoid_gate * (1.0 + gate * (1.0 - sigmoid_gate))
        gate_out_ref[spot] = (grad * up * slope).astype(jnp.bfloat16)
        up_out_ref[spot] = (grad * (gate * sigmoid_gate)).astype(jnp.bfloat16)
        for index, (source, target) in enumerate(((gate_out_ref, gate_out), (up_out_ref, up_out))):
            stores.append(
                pltpu.make_async_copy(source.at[spot], target.at[spot], store_sems.at[index, expert, part])
            )
            stores[-1].start()
    for store in stores:
        store.wait()


def gate_up_grads(own_grad, gate_pre, up_pre, after):
    parts = 2
    resident = pl.BlockSpec(memory_space=pltpu.VMEM)
    outside = pl.BlockSpec(memory_space=pltpu.HBM)
    shaped = pltpu.VMEM(gate_pre.shape, jnp.bfloat16)
    return pl.pallas_call(
        gate_up_kernel,
        in_specs=[outside, resident, resident, pl.BlockSpec(memory_space=pl.ANY)],
        out_specs=[outside, outside],
        out_shape=[pltpu.HBM(gate_pre.shape, jnp.bfloat16)] * 2,
        scratch_shapes=[
            shaped,
            shaped,
            shaped,
            pltpu.SemaphoreType.DMA((gate_pre.shape[0], parts)),
            pltpu.SemaphoreType.DMA((2, gate_pre.shape[0], parts)),
        ],
        compiler_params=pltpu.CompilerParams(vmem_limit_bytes=VMEM_GRANT),
        name="gate_up_grads",
    )(pltpu.with_memory_space_constraint(own_grad, pltpu.HBM), gate_pre, up_pre, after)


def dispatch_kernel(turn, place_ref, own_ref, other_ref, weight_ref, *refs):
    placed_out, partial_out, placed_ref, partial_ref, placed_sems, partial_sems = refs[-6:]
    sources = own_ref.shape[0]
    meta_start = own_ref.shape[1] - META
    experts_here, width, _ = weight_ref.shape
    half = meta_start * LANES // width
    tokens = 2 * half
    steps = partial_ref.shape[0]
    blocks = sources // steps
    before = lax.broadcasted_iota(jnp.int32, (tokens, tokens), 0)
    after = lax.broadcasted_iota(jnp.int32, (tokens, tokens), 1)
    earlier = (before < after).astype(jnp.bfloat16)
    slot_row = lax.broadcasted_iota(jnp.int32, (CAP, tokens), 0).astype(jnp.float32)
    plane = place_ref[turn]
    core = place_ref[4]
    first = (core * experts_here).astype(jnp.float32)
    members, probs = [], []
    for block in range(sources):
        meta = own_ref[block, meta_start : meta_start + META, :].astype(jnp.float32)
        first_id, second_id = meta[0:1], meta[1:2]
        first_prob = (meta[2:3] + meta[3:4]) + meta[4:5]
        second_prob = (meta[5:6] + meta[6:7]) + meta[7:8]
        for expert in range(experts_here):
            one = first_id == first + expert
            two = second_id == first + expert
            members.append(jnp.logical_or(one, two).astype(jnp.float32))
            probs.append(jnp.where(one, first_prob, jnp.where(two, second_prob, 0.0)))
    member = jnp.concatenate(members, axis=0)
    slots = jnp.dot(member.astype(jnp.bfloat16), earlier, preferred_element_type=jnp.float32)
    slots = jnp.where(member > 0.0, slots, -1.0)
    prob = jnp.concatenate(probs, axis=0)
    slots = jnp.where(core == 1, pltpu.roll(slots, half, 1), slots)
    prob = jnp.where(core == 1, pltpu.roll(prob, half, 1), prob)
    copies = []
    for block in range(sources):
        strips = [
            jnp.concatenate([ref[block, start : start + half, :] for ref in (own_ref, other_ref)], axis=0)
            for start in range(0, meta_start, half)
        ]
        tokens_here = jnp.concatenate(strips, axis=1)
        chosen, scales = [], []
        for expert in range(experts_here):
            line = block * experts_here + expert
            match = (slot_row == slots[line : line + 1]).astype(jnp.float32)
            chosen.append(match)
            scales.append(jnp.sum(match * prob[line : line + 1], axis=1, keepdims=True))
        picked = jnp.dot(
            jnp.concatenate(chosen, axis=0).astype(jnp.bfloat16),
            tokens_here,
            preferred_element_type=jnp.float32,
        )
        scaled = (picked * jnp.concatenate(scales, axis=0)).astype(jnp.bfloat16)
        for expert in range(experts_here):
            placed_ref[expert, block * CAP : (block + 1) * CAP, :] = scaled[expert * CAP : (expert + 1) * CAP]
        if block % 2 == 1:
            start = (block - 1) * CAP
            target = pl.multiple_of(plane * (sources * CAP) + start, 2 * CAP)
            for expert in range(experts_here):
                copies.append(
                    pltpu.make_async_copy(
                        placed_ref.at[expert, pl.ds(start, 2 * CAP), :],
                        placed_out.at[expert, pl.ds(target, 2 * CAP), :],
                        placed_sems.at[block // 2, expert],
                    )
                )
                copies[-1].start()
        if block % blocks == blocks - 1:
            step = block // blocks
            for expert in range(experts_here):
                partial_ref[step, expert] = jnp.dot(
                    placed_ref[expert, step * blocks * CAP : (step + 1) * blocks * CAP, :],
                    weight_ref[expert],
                    preferred_element_type=jnp.float32,
                ).astype(jnp.bfloat16)
                copies.append(
                    pltpu.make_async_copy(
                        partial_ref.at[step, expert],
                        partial_out.at[plane * steps + step, expert],
                        partial_sems.at[step, expert],
                    )
                )
                copies[-1].start()
    for copy in copies:
        copy.wait()


def dispatch_and_project(turn, places, own_half, other_half, weight, rows, owners, buffers):
    experts_here, width, hidden_width = weight.shape
    sources = own_half.shape[0]
    steps = 2
    per_owner = rows // owners
    resident = pl.BlockSpec(memory_space=pltpu.VMEM)
    outside = pl.BlockSpec(memory_space=pltpu.HBM)
    return pl.pallas_call(
        functools.partial(dispatch_kernel, turn),
        in_specs=[pl.BlockSpec(memory_space=pltpu.SMEM), resident, resident, resident]
        + [outside] * len(buffers),
        out_specs=[outside, outside],
        out_shape=[
            pltpu.HBM((experts_here, rows, width), jnp.bfloat16),
            pltpu.HBM((owners, experts_here, per_owner, hidden_width), jnp.bfloat16),
        ],
        scratch_shapes=[
            pltpu.VMEM((experts_here, steps * per_owner, width), jnp.bfloat16),
            pltpu.VMEM((steps, experts_here, per_owner, hidden_width), jnp.bfloat16),
            pltpu.SemaphoreType.DMA((sources // 2, experts_here)),
            pltpu.SemaphoreType.DMA((steps, experts_here)),
        ],
        input_output_aliases={4 + i: i for i in range(len(buffers))},
        compiler_params=pltpu.CompilerParams(vmem_limit_bytes=VMEM_GRANT),
        name="dispatch_project",
    )(places, own_half, other_half, weight, *buffers)


def weight_grad_kernel(hidden_ref, placed_ref, grad_ref, squares_ref, total_ref):
    expert = pl.program_id(0)
    grad = lax.dot_general(
        hidden_ref[0], placed_ref[0], (((0,), (0,)), ((), ())), preferred_element_type=jnp.float32
    )
    grad_ref[0] = grad
    squares = jnp.sum(grad * grad, axis=0, keepdims=True)

    @pl.when(expert == 0)
    def _():
        total_ref[...] = squares

    @pl.when(expert > 0)
    def _():
        total_ref[...] += squares

    @pl.when(expert == pl.num_programs(0) - 1)
    def _():
        squares_ref[...] = jnp.full(squares_ref.shape, jnp.sum(total_ref[...]), jnp.float32)


def weight_grads(hidden_all, arrived, copies):
    experts, rows, hidden_width = hidden_all.shape
    width = arrived.shape[2]
    return pl.pallas_call(
        weight_grad_kernel,
        grid=(experts,),
        in_specs=[
            pl.BlockSpec((1, rows, hidden_width), lambda i: (i, 0, 0)),
            pl.BlockSpec((1, rows, width), lambda i: (i, 0, 0)),
        ],
        out_specs=[
            pl.BlockSpec((1, hidden_width, width), lambda i: (i, 0, 0)),
            pl.BlockSpec((copies, 1, LANES), lambda i: (0, 0, 0)),
        ],
        out_shape=[
            jax.ShapeDtypeStruct((experts, hidden_width, width), jnp.float32),
            jax.ShapeDtypeStruct((copies, 1, LANES), jnp.float32),
        ],
        scratch_shapes=[pltpu.VMEM((1, width), jnp.float32)],
        compiler_params=pltpu.CompilerParams(
            dimension_semantics=("arbitrary",), vmem_limit_bytes=2 * VMEM_GRANT
        ),
        name="weight_grads",
    )(
        pltpu.with_memory_space_constraint(hidden_all, pltpu.HBM),
        pltpu.with_memory_space_constraint(arrived, pltpu.HBM),
    )


def exchange(value, axis):
    return lax.all_to_all(value, axis, 0, 0, tiled=True)


def to_all(value, axis):
    return exchange(jnp.broadcast_to(value[None], (lax.axis_size(axis),) + value.shape), axis)


def swap_cores(value):
    return lax.ppermute(value, "expert", [(0, 1), (1, 0)])


def along_x(value):
    size = lax.axis_size("x")
    pairs = []
    for place in range(size):
        pairs.append((place * 2, (place + 1) % size * 2))
        pairs.append((place * 2 + 1, (place - 1) % size * 2 + 1))
    return lax.ppermute(value, ("x", "expert"), pairs)


def on_device(grad_rows, gate_probs, expert_ids, gate_pre, up_pre, down_weight):
    experts_here, rows_here, hidden_width = gate_pre.shape
    tokens_here, feature_width = grad_rows.shape
    cores = lax.axis_size("expert")
    planes = lax.axis_size("x")
    lines = lax.axis_size("y")
    sources = planes * lines
    owners = lax.axis_size("ffn")
    experts_total = experts_here * cores
    core = lax.axis_index("expert")
    plane = lax.axis_index("x")
    rows = rows_here * owners

    payload, hidden = prepare(core, grad_rows, expert_ids, gate_probs, gate_pre, up_pre, lines)
    near = exchange(payload, "y")
    hidden_all = lax.all_gather(hidden, "ffn", axis=1, tiled=True)
    weight = jnp.swapaxes(down_weight, 1, 2)
    offsets = [0, planes - 1 + 2 * core, 1 + planes - 2 * core, 2]
    places = jnp.stack([(plane + offset) % planes for offset in offsets] + [core]).astype(jnp.int32)

    def project(turn, own_half, other_half, buffers):
        return dispatch_and_project(
            turn, places, own_half, other_half, weight, rows, owners, buffers
        )

    side_own = along_x(near)
    near_other = swap_cores(near)
    side_other = along_x(near_other)
    buffers = project(0, near, near_other, ())
    side_own, buffers = lax.optimization_barrier((side_own, buffers))
    far_own = along_x(side_own)
    beyond_other = swap_cores(side_own)
    beyond_own = swap_cores(side_other)
    buffers = project(1, side_own, side_other, buffers)
    far_own, buffers = lax.optimization_barrier((far_own, buffers))
    far_other = swap_cores(far_own)
    buffers = project(2, beyond_own, beyond_other, buffers)
    arrived, partial_terms = project(3, far_own, far_other, buffers)
    own_grad = lax.psum_scatter(partial_terms, "ffn", scatter_dimension=0, tiled=True)[0]

    weight_grad, squares = weight_grads(hidden_all, arrived, sources)
    squares = jnp.sum(exchange(squares, ("x", "y")), axis=0)
    squares = jnp.sum(to_all(squares, ("expert", "ffn"))[:, 0, 0])
    entry_count = (
        float(experts_total) * float(hidden_width * sources) * float(feature_width * owners)
    )
    clip_limit = jnp.float32(0.5 * math.sqrt(entry_count))
    factor = clip_limit / jnp.maximum(jnp.sqrt(squares), clip_limit)
    down_grad = (weight_grad * factor).astype(jnp.bfloat16)

    gate_grad, up_grad = gate_up_grads(own_grad, gate_pre, up_pre, down_grad)
    return (down_grad, gate_grad, up_grad)


def solution(mesh):
    fine = Mesh(mesh.devices.reshape((X_CHIPS, -1) + mesh.devices.shape[1:]), ("x", "y", "expert", "ffn"))
    spread = ("x", "y")
    placed = (
        P(spread, "ffn"),
        P(spread, None),
        P(spread, None),
        P("expert", "ffn", spread),
        P("expert", "ffn", spread),
        P("expert", spread, "ffn"),
    )
    return jax.shard_map(
        on_device,
        mesh=fine,
        in_specs=placed,
        out_specs=(P("expert", spread, "ffn"), P("expert", "ffn", spread), P("expert", "ffn", spread)),
        check_vma=False,
    )
```

```python
import functools
import math

import jax
import jax.numpy as jnp
from jax import lax
from jax.experimental import pallas as pl
from jax.experimental.pallas import tpu as pltpu
from jax.sharding import Mesh
from jax.sharding import PartitionSpec as P

CAP = 72
META = 8
LANES = 128
X_CHIPS = 4
VMEM_GRANT = 16 * 2**20


def prepare_kernel(core_ref, rows_ref, ids_ref, probs_ref, gate_ref, up_ref, payload_ref, hidden_ref):
    lanes = payload_ref.shape[2]
    half = rows_ref.shape[0] // 2
    rows = rows_ref[pl.ds(core_ref[0] * half, half), :]
    probs = probs_ref[...]
    high = probs.astype(jnp.bfloat16).astype(jnp.float32)
    middle = (probs - high).astype(jnp.bfloat16).astype(jnp.float32)
    low = (probs - high) - middle
    lines = [ids_ref[...].astype(jnp.float32)]
    for route in range(probs.shape[0]):
        lines += [piece[route : route + 1] for piece in (high, middle, low)]
    meta = jnp.concatenate(lines, axis=0).astype(jnp.bfloat16)
    strips = [rows[:, start : start + lanes] for start in range(0, rows.shape[1], lanes)]
    payload = jnp.concatenate(strips + [meta], axis=0)
    for copy in range(payload_ref.shape[0]):
        payload_ref[copy] = payload
    gate = gate_ref[...].astype(jnp.float32)
    up = up_ref[...].astype(jnp.float32)
    hidden_ref[...] = (gate * jax.nn.sigmoid(gate) * up).astype(jnp.bfloat16)


def prepare(core, grad_rows, expert_ids, gate_probs, gate_pre, up_pre, copies):
    tokens, width = grad_rows.shape
    padded = tokens * width // (2 * LANES) + META
    operands = (grad_rows, expert_ids.T, gate_probs.T, gate_pre, up_pre)
    results = [
        jax.ShapeDtypeStruct((copies, padded, LANES), jnp.bfloat16),
        jax.ShapeDtypeStruct(gate_pre.shape, jnp.bfloat16),
    ]

    def whole(array):
        zeros = (0,) * len(array.shape)
        return pl.BlockSpec(array.shape, lambda i: zeros)

    return pl.pallas_call(
        prepare_kernel,
        grid=(1,),
        in_specs=[pl.BlockSpec(memory_space=pltpu.SMEM)] + [whole(operand) for operand in operands],
        out_specs=[whole(result) for result in results],
        out_shape=results,
        name="prepare",
    )(core.reshape(1), *operands)


def gate_up_kernel(grad_ref, gate_ref, up_ref, after_ref, gate_out_ref, up_out_ref):
    gate = gate_ref[0].astype(jnp.float32)
    up = up_ref[0].astype(jnp.float32)
    grad = grad_ref[0].astype(jnp.float32)
    sigmoid_gate = jax.nn.sigmoid(gate)
    gate_out_ref[0] = (grad * up * sigmoid_gate * (1.0 + gate * (1.0 - sigmoid_gate))).astype(jnp.bfloat16)
    up_out_ref[0] = (grad * (gate * sigmoid_gate)).astype(jnp.bfloat16)


def gate_up_grads(own_grad, gate_pre, up_pre, after):
    experts, rows, width = gate_pre.shape
    block = pl.BlockSpec((1, rows, width), lambda i: (i, 0, 0))
    return pl.pallas_call(
        gate_up_kernel,
        grid=(experts,),
        in_specs=[block, block, block, pl.BlockSpec(memory_space=pl.ANY)],
        out_specs=[block, block],
        out_shape=[pltpu.HBM(gate_pre.shape, jnp.bfloat16)] * 2,
        compiler_params=pltpu.CompilerParams(vmem_limit_bytes=VMEM_GRANT),
        name="gate_up_grads",
    )(pltpu.with_memory_space_constraint(own_grad, pltpu.HBM), gate_pre, up_pre, after)


def dispatch_kernel(turn, place_ref, own_ref, other_ref, weight_ref, *refs):
    placed_out, partial_out, placed_ref, partial_ref, placed_sems, partial_sems = refs[-6:]
    sources = own_ref.shape[0]
    meta_start = own_ref.shape[1] - META
    experts_here, width, _ = weight_ref.shape
    half = meta_start * LANES // width
    tokens = 2 * half
    steps = partial_ref.shape[0]
    blocks = sources // steps
    before = lax.broadcasted_iota(jnp.int32, (tokens, tokens), 0)
    after = lax.broadcasted_iota(jnp.int32, (tokens, tokens), 1)
    earlier = (before < after).astype(jnp.bfloat16)
    slot_row = lax.broadcasted_iota(jnp.int32, (CAP, tokens), 0).astype(jnp.float32)
    plane = place_ref[turn]
    core = place_ref[4]
    first = (core * experts_here).astype(jnp.float32)
    members, probs = [], []
    for block in range(sources):
        meta = own_ref[block, meta_start : meta_start + META, :].astype(jnp.float32)
        first_id, second_id = meta[0:1], meta[1:2]
        first_prob = (meta[2:3] + meta[3:4]) + meta[4:5]
        second_prob = (meta[5:6] + meta[6:7]) + meta[7:8]
        for expert in range(experts_here):
            one = first_id == first + expert
            two = second_id == first + expert
            members.append(jnp.logical_or(one, two).astype(jnp.float32))
            probs.append(jnp.where(one, first_prob, jnp.where(two, second_prob, 0.0)))
    member = jnp.concatenate(members, axis=0)
    slots = jnp.dot(member.astype(jnp.bfloat16), earlier, preferred_element_type=jnp.float32)
    slots = jnp.where(member > 0.0, slots, -1.0)
    prob = jnp.concatenate(probs, axis=0)
    slots = jnp.where(core == 1, pltpu.roll(slots, half, 1), slots)
    prob = jnp.where(core == 1, pltpu.roll(prob, half, 1), prob)
    copies = []
    for block in range(sources):
        strips = [
            jnp.concatenate([ref[block, start : start + half, :] for ref in (own_ref, other_ref)], axis=0)
            for start in range(0, meta_start, half)
        ]
        tokens_here = jnp.concatenate(strips, axis=1)
        chosen, scales = [], []
        for expert in range(experts_here):
            line = block * experts_here + expert
            match = (slot_row == slots[line : line + 1]).astype(jnp.float32)
            chosen.append(match)
            scales.append(jnp.sum(match * prob[line : line + 1], axis=1, keepdims=True))
        picked = jnp.dot(
            jnp.concatenate(chosen, axis=0).astype(jnp.bfloat16),
            tokens_here,
            preferred_element_type=jnp.float32,
        )
        scaled = (picked * jnp.concatenate(scales, axis=0)).astype(jnp.bfloat16)
        for expert in range(experts_here):
            placed_ref[expert, block * CAP : (block + 1) * CAP, :] = scaled[expert * CAP : (expert + 1) * CAP]
        if block % 2 == 1:
            start = (block - 1) * CAP
            target = pl.multiple_of(plane * (sources * CAP) + start, 2 * CAP)
            for expert in range(experts_here):
                copies.append(
                    pltpu.make_async_copy(
                        placed_ref.at[expert, pl.ds(start, 2 * CAP), :],
                        placed_out.at[expert, pl.ds(target, 2 * CAP), :],
                        placed_sems.at[block // 2, expert],
                    )
                )
                copies[-1].start()
        if block % blocks == blocks - 1:
            step = block // blocks
            for expert in range(experts_here):
                partial_ref[step, expert] = jnp.dot(
                    placed_ref[expert, step * blocks * CAP : (step + 1) * blocks * CAP, :],
                    weight_ref[expert],
                    preferred_element_type=jnp.float32,
                ).astype(jnp.bfloat16)
                copies.append(
                    pltpu.make_async_copy(
                        partial_ref.at[step, expert],
                        partial_out.at[plane * steps + step, expert],
                        partial_sems.at[step, expert],
                    )
                )
                copies[-1].start()
    for copy in copies:
        copy.wait()


def dispatch_and_project(turn, places, own_half, other_half, weight, rows, owners, buffers):
    experts_here, width, hidden_width = weight.shape
    sources = own_half.shape[0]
    steps = 2
    per_owner = rows // owners
    resident = pl.BlockSpec(memory_space=pltpu.VMEM)
    outside = pl.BlockSpec(memory_space=pltpu.HBM)
    return pl.pallas_call(
        functools.partial(dispatch_kernel, turn),
        in_specs=[pl.BlockSpec(memory_space=pltpu.SMEM), resident, resident, resident]
        + [outside] * len(buffers),
        out_specs=[outside, outside],
        out_shape=[
            pltpu.HBM((experts_here, rows, width), jnp.bfloat16),
            pltpu.HBM((owners, experts_here, per_owner, hidden_width), jnp.bfloat16),
        ],
        scratch_shapes=[
            pltpu.VMEM((experts_here, steps * per_owner, width), jnp.bfloat16),
            pltpu.VMEM((steps, experts_here, per_owner, hidden_width), jnp.bfloat16),
            pltpu.SemaphoreType.DMA((sources // 2, experts_here)),
            pltpu.SemaphoreType.DMA((steps, experts_here)),
        ],
        input_output_aliases={4 + i: i for i in range(len(buffers))},
        compiler_params=pltpu.CompilerParams(vmem_limit_bytes=VMEM_GRANT),
        name="dispatch_project",
    )(places, own_half, other_half, weight, *buffers)


def weight_grad_kernel(hidden_ref, placed_ref, grad_ref, squares_ref, total_ref):
    expert = pl.program_id(0)
    grad = lax.dot_general(
        hidden_ref[0], placed_ref[0], (((0,), (0,)), ((), ())), preferred_element_type=jnp.float32
    )
    grad_ref[0] = grad
    squares = jnp.sum(grad * grad, axis=0, keepdims=True)

    @pl.when(expert == 0)
    def _():
        total_ref[...] = squares

    @pl.when(expert > 0)
    def _():
        total_ref[...] += squares

    @pl.when(expert == pl.num_programs(0) - 1)
    def _():
        squares_ref[...] = jnp.full(squares_ref.shape, jnp.sum(total_ref[...]), jnp.float32)


def weight_grads(hidden_all, arrived, copies):
    experts, rows, hidden_width = hidden_all.shape
    width = arrived.shape[2]
    return pl.pallas_call(
        weight_grad_kernel,
        grid=(experts,),
        in_specs=[
            pl.BlockSpec((1, rows, hidden_width), lambda i: (i, 0, 0)),
            pl.BlockSpec((1, rows, width), lambda i: (i, 0, 0)),
        ],
        out_specs=[
            pl.BlockSpec((1, hidden_width, width), lambda i: (i, 0, 0)),
            pl.BlockSpec((copies, 1, LANES), lambda i: (0, 0, 0)),
        ],
        out_shape=[
            jax.ShapeDtypeStruct((experts, hidden_width, width), jnp.float32),
            jax.ShapeDtypeStruct((copies, 1, LANES), jnp.float32),
        ],
        scratch_shapes=[pltpu.VMEM((1, width), jnp.float32)],
        compiler_params=pltpu.CompilerParams(
            dimension_semantics=("arbitrary",), vmem_limit_bytes=2 * VMEM_GRANT
        ),
        name="weight_grads",
    )(
        pltpu.with_memory_space_constraint(hidden_all, pltpu.HBM),
        pltpu.with_memory_space_constraint(arrived, pltpu.HBM),
    )


def exchange(value, axis):
    return lax.all_to_all(value, axis, 0, 0, tiled=True)


def to_all(value, axis):
    return exchange(jnp.broadcast_to(value[None], (lax.axis_size(axis),) + value.shape), axis)


def swap_cores(value):
    return lax.ppermute(value, "expert", [(0, 1), (1, 0)])


def along_x(value):
    size = lax.axis_size("x")
    pairs = []
    for place in range(size):
        pairs.append((place * 2, (place + 1) % size * 2))
        pairs.append((place * 2 + 1, (place - 1) % size * 2 + 1))
    return lax.ppermute(value, ("x", "expert"), pairs)


def on_device(grad_rows, gate_probs, expert_ids, gate_pre, up_pre, down_weight):
    experts_here, rows_here, hidden_width = gate_pre.shape
    tokens_here, feature_width = grad_rows.shape
    cores = lax.axis_size("expert")
    planes = lax.axis_size("x")
    lines = lax.axis_size("y")
    sources = planes * lines
    owners = lax.axis_size("ffn")
    experts_total = experts_here * cores
    core = lax.axis_index("expert")
    plane = lax.axis_index("x")
    rows = rows_here * owners

    payload, hidden = prepare(core, grad_rows, expert_ids, gate_probs, gate_pre, up_pre, lines)
    near = exchange(payload, "y")
    hidden_all = lax.all_gather(hidden, "ffn", axis=1, tiled=True)
    offsets = [0, planes - 1 + 2 * core, 1 + planes - 2 * core, 2]
    places = jnp.stack([(plane + offset) % planes for offset in offsets] + [core]).astype(jnp.int32)

    def project(turn, own_half, other_half, buffers):
        return dispatch_and_project(
            turn, places, own_half, other_half, weight, rows, owners, buffers
        )

    side_own = along_x(near)
    near_other = swap_cores(near)
    side_other = along_x(near_other)
    side_own, down_weight = lax.optimization_barrier((side_own, down_weight))
    weight = jnp.swapaxes(down_weight, 1, 2)
    buffers = project(0, near, near_other, ())
    far_own = along_x(side_own)
    beyond_other = swap_cores(side_own)
    beyond_own = swap_cores(side_other)
    buffers = project(1, side_own, side_other, buffers)
    far_own, buffers = lax.optimization_barrier((far_own, buffers))
    far_other = swap_cores(far_own)
    buffers = project(2, beyond_own, beyond_other, buffers)
    arrived, partial_terms = project(3, far_own, far_other, buffers)
    own_grad = lax.psum_scatter(partial_terms, "ffn", scatter_dimension=0, tiled=True)[0]

    weight_grad, squares = weight_grads(hidden_all, arrived, sources)
    squares = jnp.sum(exchange(squares, ("x", "y")), axis=0)
    squares = jnp.sum(to_all(squares, ("expert", "ffn"))[:, 0, 0])
    entry_count = (
        float(experts_total) * float(hidden_width * sources) * float(feature_width * owners)
    )
    clip_limit = jnp.float32(0.5 * math.sqrt(entry_count))
    factor = clip_limit / jnp.maximum(jnp.sqrt(squares), clip_limit)
    down_grad = (weight_grad * factor).astype(jnp.bfloat16)

    gate_grad, up_grad = gate_up_grads(own_grad, gate_pre, up_pre, down_grad)
    return (down_grad, gate_grad, up_grad)


def solution(mesh):
    fine = Mesh(mesh.devices.reshape((X_CHIPS, -1) + mesh.devices.shape[1:]), ("x", "y", "expert", "ffn"))
    spread = ("x", "y")
    placed = (
        P(spread, "ffn"),
        P(spread, None),
        P(spread, None),
        P("expert", "ffn", spread),
        P("expert", "ffn", spread),
        P("expert", spread, "ffn"),
    )
    return jax.shard_map(
        on_device,
        mesh=fine,
        in_specs=placed,
        out_specs=(P("expert", spread, "ffn"), P("expert", "ffn", spread), P("expert", "ffn", spread)),
        check_vma=False,
    )
```
